32 devices in a mesh: fsdp: 8 (over z, y), tensor: 4 (over x, core).
Axes of the slice: x: 2, y: 2, z: 4, core: 2. Of those that a mesh axis runs over, the one named last changes fastest.
Arguments:
- block_input: bfloat16 [16, 197, 768], P('fsdp'), may hold values from -6 to 6
- output_grad: bfloat16 [16, 197, 768], P('fsdp'), may hold values from -6 to 6
- live_images: int32 [16], P('fsdp'), may hold values from 0 to 1, as said below
- w_qkv: float32 [768, 3, 768], P('fsdp', None, 'tensor'), may hold values from -6 to 6
- w_out: float32 [768, 768], P('tensor', 'fsdp'), may hold values from -0.625 to 0.625
- w_fc1: float32 [768, 3072], P('fsdp', 'tensor'), may hold values from -0.21875 to 0.21875
- w_fc2: float32 [3072, 768], P('tensor', 'fsdp'), may hold values from -0.109375 to 0.109375
- qv_bias: float32 [2, 12, 64], P(None, 'tensor', 'fsdp'), may hold values from -1.2 to 1.2
- fc1_bias: float32 [48, 64], P('tensor', 'fsdp'), may hold values from -1.2 to 1.2
- norm_vec: float32 [6, 768], P(None, 'fsdp'), may hold values from -0.9 to 1.5
- mom_qkv: float32 [2, 768, 3, 768], P(None, 'fsdp', None, 'tensor'), may hold values from -5.0528408 to 5.0528408, as said below
- mom_out: float32 [2, 768, 768], P(None, 'tensor', 'fsdp'), may hold values from -5.0528408 to 5.0528408, as said below
- mom_fc1: float32 [2, 768, 3072], P(None, 'fsdp', 'tensor'), may hold values from -5.0528408 to 5.0528408, as said below
- mom_fc2: float32 [2, 3072, 768], P(None, 'tensor', 'fsdp'), may hold values from -5.0528408 to 5.0528408, as said below
- mom_qvb: float32 [2, 2, 12, 64], P(None, None, 'tensor', 'fsdp'), may hold values from -5.0528408 to 5.0528408, as said below
- mom_fc1b: float32 [2, 48, 64], P(None, 'tensor', 'fsdp'), may hold values from -5.0528408 to 5.0528408, as said below
- mom_vec: float32 [2, 6, 768], P(None, None, 'fsdp'), may hold values from -5.0528408 to 5.0528408, as said below
Outputs:
- block_output: bfloat16 [16, 197, 768], P('fsdp')
- input_grad: float32 [16, 197, 768], P('fsdp')
- grad_qkv: float32 [768, 3, 768], P('fsdp', None, 'tensor')
- grad_out: float32 [768, 768], P('tensor', 'fsdp')
- grad_fc1: float32 [768, 3072], P('fsdp', 'tensor')
- grad_fc2: float32 [3072, 768], P('tensor', 'fsdp')
- grad_qvb: float32 [2, 12, 64], P(None, 'tensor', 'fsdp')
- grad_fc1b: float32 [48, 64], P('tensor', 'fsdp')
- grad_vec: float32 [6, 768], P(None, 'fsdp')
- new_qkv: float32 [768, 3, 768], P('fsdp', None, 'tensor')
- new_out: float32 [768, 768], P('tensor', 'fsdp')
- new_fc1: float32 [768, 3072], P('fsdp', 'tensor')
- new_fc2: float32 [3072, 768], P('tensor', 'fsdp')
- new_qvb: float32 [2, 12, 64], P(None, 'tensor', 'fsdp')
- new_fc1b: float32 [48, 64], P('tensor', 'fsdp')
- new_vec: float32 [6, 768], P(None, 'fsdp')
- newmom_qkv: float32 [2, 768, 3, 768], P(None, 'fsdp', None, 'tensor')
- newmom_out: float32 [2, 768, 768], P(None, 'tensor', 'fsdp')
- newmom_fc1: float32 [2, 768, 3072], P(None, 'fsdp', 'tensor')
- newmom_fc2: float32 [2, 3072, 768], P(None, 'tensor', 'fsdp')
- newmom_qvb: float32 [2, 2, 12, 64], P(None, None, 'tensor', 'fsdp')
- newmom_fc1b: float32 [2, 48, 64], P(None, 'tensor', 'fsdp')
- newmom_vec: float32 [2, 6, 768], P(None, None, 'fsdp')
The draws below stay inside these ranges and needn't reach their ends.
Inputs may be any that keep to these rules, and one draw needn't show every extreme that they name: `live_images`: in each aligned block of 2 slots (those of one index of fsdp) either all images are live or exactly one slot is empty; blocks of both kinds occur in every draw. `mom_qkv`: the second moments are positive. `mom_out`: the second moments are positive. `mom_fc1`: the second moments are positive. `mom_fc2`: the second moments are positive. `mom_qvb`: the second moments are positive. `mom_fc1b`: the second moments are positive. `mom_vec`: the second moments are positive.
All inputs are finite; a program needn't handle non-finite values.
Results may differ from the reference program's by a relative error of at most 0.017.
Values may be sent and summed in bfloat16 or wider, within the bound.
A program may use at most 64 MiB of HBM per device.

```python
import math
import jax
import jax.numpy as jnp
from jax import lax

D = 768
HEADS = 12
HD = 64
FF = 3072
SEQ = 197
SLOTS = 2
IMAGES = 16
TOKENS = 3152
N_FSDP = 8
N_TENSOR = 4


def draw_live_images(key, part):
    devices = IMAGES // SLOTS
    short = jax.random.randint(jax.random.fold_in(key, 11), (devices,), 0, 2)
    short = short.at[0].set(0).at[1].set(1)
    gap = jax.random.randint(jax.random.fold_in(key, 12), (devices,), 0, SLOTS)
    slot_ids = jnp.arange(SLOTS, dtype=jnp.int32)
    empty = (short[:, None] == 1) & (slot_ids[None, :] == gap[:, None])
    return jnp.where(empty, 0, 1).astype(jnp.int32).reshape(IMAGES)


def draw_w_qkv(key, part):
    base = jax.random.truncated_normal(jax.random.fold_in(key, 21), -4.0, 4.0, (D, 3, D), jnp.float32) * D ** (-0.5)
    return base


def draw_norm_vec(key, part):
    gains = jax.random.uniform(jax.random.fold_in(key, 31), (6, D), jnp.float32, 0.5, 1.5)
    shifts = jax.random.truncated_normal(jax.random.fold_in(key, 32), -3.0, 3.0, (6, D), jnp.float32) * 0.3
    row_ids = jnp.arange(6)
    is_gain = (row_ids % 2 == 0) & (row_ids < 4)
    return jnp.where(is_gain[:, None], gains, shifts)


def moment_pair(key, shape, marker):
    own_key = jax.random.fold_in(key, marker)
    first = jax.random.truncated_normal(jax.random.fold_in(own_key, 41), -3.0, 3.0, shape, jnp.float32) * (0.03 * TOKENS ** 0.5)
    spread = jax.random.uniform(jax.random.fold_in(own_key, 42), shape, jnp.float32, math.log(0.3), math.log(3.0))
    second = jnp.exp(spread) * (0.0003 * TOKENS)
    return jnp.stack([first, second])


def draw_mom_qkv(key, part):
    return moment_pair(key, (D, 3, D), 51)


def draw_mom_out(key, part):
    return moment_pair(key, (D, D), 52)


def draw_mom_fc1(key, part):
    return moment_pair(key, (D, FF), 53)


def draw_mom_fc2(key, part):
    return moment_pair(key, (FF, D), 54)


def draw_mom_qvb(key, part):
    return moment_pair(key, (2, HEADS, HD), 55)


def draw_mom_fc1b(key, part):
    return moment_pair(key, (FF // HD, HD), 56)


def draw_mom_vec(key, part):
    return moment_pair(key, (6, D), 57)


def levels(stream_key, dims, shards, low, high):
    level, own = 1.0, jax.random.fold_in(stream_key, 6)
    for dim, blocks in shards:
        draws = jnp.exp(jax.random.uniform(jax.random.fold_in(own, dim), (blocks,), jnp.float32, low / len(shards), high / len(shards)))
        level = level * jnp.repeat(draws, dims[dim] // blocks).reshape([-1 if axis == dim else 1 for axis in range(len(dims))])
    return level


def gaussian(key, dims, scale, limit, split=(), kind=jnp.bfloat16):
    values = scale * jax.random.normal(key, dims, jnp.float32)
    if split:
        values = values * levels(key, dims, split, -0.22, 0.18)
    return jnp.clip(values, -limit, limit).astype(kind)


def setup_inputs(seed: int = 0) -> dict:
    seeds = jax.random.split(jax.random.key(seed), 18)
    block_input = gaussian(seeds[0], (IMAGES, SEQ, D), 1.0, 6.0, ((0, 8),))
    output_grad = gaussian(seeds[1], (IMAGES, SEQ, D), 1.0, 6.0, ((0, 8),))
    live_images = draw_live_images(jax.random.fold_in(seeds[17], 71), 0)
    w_qkv = draw_w_qkv(jax.random.fold_in(seeds[17], 71), 0)
    w_out = gaussian(seeds[4], (D, D), (D // 8) ** -0.5, 0.625, ((0, 4), (1, 8)), jnp.float32)
    w_fc1 = gaussian(seeds[5], (D, FF), D ** -0.5, 0.21875, ((0, 8), (1, 4)), jnp.float32)
    w_fc2 = gaussian(seeds[6], (FF, D), FF ** -0.5, 0.109375, ((0, 4), (1, 8)), jnp.float32)
    qv_bias = gaussian(seeds[7], (2, HEADS, HD), 0.3, 1.2, ((1, 4), (2, 8)), jnp.float32)
    fc1_bias = gaussian(seeds[8], (FF // HD, HD), 0.3, 1.2, ((0, 4), (1, 8)), jnp.float32)
    norm_vec = draw_norm_vec(jax.random.fold_in(seeds[17], 71), 0)
    mom_qkv = draw_mom_qkv(jax.random.fold_in(seeds[17], 71), 0)
    mom_out = draw_mom_out(jax.random.fold_in(seeds[17], 71), 0)
    mom_fc1 = draw_mom_fc1(jax.random.fold_in(seeds[17], 71), 0)
    mom_fc2 = draw_mom_fc2(jax.random.fold_in(seeds[17], 71), 0)
    mom_qvb = draw_mom_qvb(jax.random.fold_in(seeds[17], 71), 0)
    mom_fc1b = draw_mom_fc1b(jax.random.fold_in(seeds[17], 71), 0)
    mom_vec = draw_mom_vec(jax.random.fold_in(seeds[17], 71), 0)
    return dict(block_input=block_input, output_grad=output_grad, live_images=live_images, w_qkv=w_qkv, w_out=w_out, w_fc1=w_fc1, w_fc2=w_fc2, qv_bias=qv_bias, fc1_bias=fc1_bias, norm_vec=norm_vec, mom_qkv=mom_qkv, mom_out=mom_out, mom_fc1=mom_fc1, mom_fc2=mom_fc2, mom_qvb=mom_qvb, mom_fc1b=mom_fc1b, mom_vec=mom_vec)


epsilon = 1e-06
sqrt_half = 0.7071067811865476
inv_root = 0.3989422804014327
corr_one = 1.0 - 0.9 ** 3
corr_two = 1.0 - 0.999 ** 3

def widen_copy(values):
    return lax.optimization_barrier(values.astype(jnp.bfloat16)).astype(jnp.float32)

def norm_forward(values, gain, shift):
    center = values - lax.optimization_barrier(jnp.mean(values, axis=-1, keepdims=True))
    variance = lax.optimization_barrier(jnp.mean(center * center, axis=-1, keepdims=True))
    scale = lax.rsqrt(variance + epsilon)
    normed = center * scale
    return (normed * gain + shift, normed, scale)

def norm_backward(upstream, normed, scale, gain):
    scaled = upstream * gain
    return scale * (scaled - lax.optimization_barrier(jnp.mean(scaled, axis=-1, keepdims=True)) - normed * lax.optimization_barrier(jnp.mean(scaled * normed, axis=-1, keepdims=True)))

def gelu_slope(pre_act):
    return 0.5 * (1.0 + lax.erf(pre_act * sqrt_half)) + pre_act * jnp.exp(-0.5 * pre_act * pre_act) * inv_root

def grouped(left, right, parts):
    count, inner = left.shape
    left_g = left.astype(jnp.float32).reshape(count, parts, inner // parts)
    right_g = right.astype(jnp.float32).reshape(parts, inner // parts, right.shape[1])
    terms = jnp.einsum('ngk,gkm->gnm', left_g, right_g).astype(jnp.bfloat16)
    terms = lax.optimization_barrier(terms)
    return lax.optimization_barrier(jnp.sum(terms.astype(jnp.float32), axis=0))

def grouped_three(upstream, weight, parts):
    count = upstream.shape[0]
    width = weight.shape[0]
    up_g = upstream.astype(jnp.float32).reshape(count, 3, parts, width // parts)
    weight_g = weight.astype(jnp.float32).reshape(width, 3, parts, width // parts)
    terms = jnp.einsum('ncgj,dcgj->gnd', up_g, weight_g).astype(jnp.bfloat16)
    terms = lax.optimization_barrier(terms)
    return lax.optimization_barrier(jnp.sum(terms.astype(jnp.float32), axis=0))

def attend(queries, key_rows, value_rows):
    scores = jnp.einsum('bqhe,bkhe->bhqk', queries.astype(jnp.float32), key_rows.astype(jnp.float32)) * 0.125
    logsum = jax.nn.logsumexp(scores, axis=-1, keepdims=True)
    probs = jnp.exp(scores - logsum).astype(jnp.bfloat16)
    mixed = jnp.einsum('bhqk,bkhe->bqhe', probs.astype(jnp.float32), value_rows.astype(jnp.float32))
    return (mixed.astype(jnp.bfloat16), logsum)

def attend_back(queries, key_rows, value_rows, logsum, upstream):
    qf = queries.astype(jnp.float32)
    kf = key_rows.astype(jnp.float32)
    vf = value_rows.astype(jnp.float32)
    uf = upstream.astype(jnp.float32)
    scores = jnp.einsum('bqhe,bkhe->bhqk', qf, kf) * 0.125
    probs = jnp.exp(scores - logsum)
    probs_low = probs.astype(jnp.bfloat16).astype(jnp.float32)
    dprobs = jnp.einsum('bqhe,bkhe->bhqk', uf, vf)
    dscore = (probs * (dprobs - lax.optimization_barrier(jnp.sum(probs * dprobs, axis=-1, keepdims=True)))).astype(jnp.bfloat16).astype(jnp.float32)
    dquery = 0.125 * jnp.einsum('bhqk,bkhe->bqhe', dscore, kf)
    dkey = 0.125 * jnp.einsum('bhqk,bqhe->bkhe', dscore, qf)
    dvalue = jnp.einsum('bhqk,bqhe->bkhe', probs_low, uf)
    return (dquery, dkey, dvalue)

def adamw(param, grad, moments):
    first = 0.9 * moments[0] + 0.1 * grad
    second = 0.999 * moments[1] + 0.001 * grad * grad
    fresh = param - 0.004 * (first / corr_one / (jnp.sqrt(second / corr_two) + 1e-08) + 0.05 * param)
    return (fresh, jnp.stack([first, second]))

def reference(block_input, output_grad, live_images, w_qkv, w_out, w_fc1, w_fc2, qv_bias, fc1_bias, norm_vec, mom_qkv, mom_out, mom_fc1, mom_fc2, mom_qvb, mom_fc1b, mom_vec):
    low = jnp.bfloat16
    inward = w_qkv.astype(low)
    outward = w_out.astype(low)
    widen = w_fc1.astype(low)
    narrow = w_fc2.astype(low)
    heads_bias = widen_copy(qv_bias).reshape(2, D)
    hidden_bias = widen_copy(fc1_bias).reshape(FF)
    vecf = widen_copy(norm_vec)
    rows = SLOTS * SEQ

    def one_block(carry, item):
        image_rows, grad_rows, live_blk = item
        flat = image_rows.astype(jnp.float32).reshape(rows, D)
        first_norm, unit_one, scale_one = norm_forward(flat, vecf[0], vecf[1])
        normed_one = first_norm.astype(low)
        projected = jnp.einsum('nd,dcj->ncj', normed_one.astype(jnp.float32), inward.astype(jnp.float32))
        shifts = jnp.stack([heads_bias[0], jnp.zeros((D,), jnp.float32), heads_bias[1]])
        triple = (projected + shifts).astype(low).reshape(SLOTS, SEQ, 3, HEADS, HD)
        queries = triple[:, :, 0]
        key_rows = triple[:, :, 1]
        value_rows = triple[:, :, 2]
        mixed, logsum = attend(queries, key_rows, value_rows)
        attn_rows = mixed.reshape(rows, D)
        resid = flat + grouped(attn_rows, outward, N_TENSOR) + vecf[4]
        second_norm, unit_two, scale_two = norm_forward(resid, vecf[2], vecf[3])
        normed_two = second_norm.astype(low)
        pre_act = jnp.dot(normed_two, widen, preferred_element_type=jnp.float32) + hidden_bias
        activ = jax.nn.gelu(pre_act, approximate=False).astype(low)
        mlp_total = grouped(activ, narrow, N_TENSOR)
        row_mask = jnp.broadcast_to(live_blk.astype(jnp.float32)[:, None], (SLOTS, SEQ)).reshape(rows, 1)
        out_rows = (row_mask * (resid + mlp_total + vecf[5])).astype(low)
        grad_flat = grad_rows.astype(jnp.float32).reshape(rows, D) * row_mask
        grad_low = grad_flat.astype(low)
        grad_narrow = jnp.einsum('nf,nd->fd', activ.astype(jnp.float32), grad_low.astype(jnp.float32))
        delta_act = jnp.einsum('nd,fd->nf', grad_low.astype(jnp.float32), narrow.astype(jnp.float32))
        delta_pre = delta_act * gelu_slope(pre_act)
        delta_pre_low = delta_pre.astype(low)
        grad_hidden = lax.optimization_barrier(jnp.sum(delta_pre, axis=0))
        grad_widen = jnp.einsum('nd,nf->df', normed_two.astype(jnp.float32), delta_pre_low.astype(jnp.float32))
        delta_two = grouped(delta_pre_low, widen.T, N_TENSOR)
        delta_resid = grad_flat + norm_backward(delta_two, unit_two, scale_two, vecf[2])
        delta_resid_low = delta_resid.astype(low)
        grad_outward = jnp.einsum('nj,nd->jd', attn_rows.astype(jnp.float32), delta_resid_low.astype(jnp.float32))
        delta_mixed = jnp.einsum('nd,jd->nj', delta_resid_low.astype(jnp.float32), outward.astype(jnp.float32))
        delta_mixed = delta_mixed.astype(low).reshape(SLOTS, SEQ, HEADS, HD)
        delta_query, delta_key, delta_value = attend_back(queries, key_rows, value_rows, logsum, delta_mixed)
        delta_triple = jnp.stack([delta_query, delta_key, delta_value], axis=2).reshape(rows, 3, D)
        grad_heads = jnp.stack([lax.optimization_barrier(jnp.sum(delta_triple[:, 0], axis=0)), lax.optimization_barrier(jnp.sum(delta_triple[:, 2], axis=0))])
        triple_low = delta_triple.astype(low)
        grad_inward = jnp.einsum('nd,ncj->dcj', normed_one.astype(jnp.float32), triple_low.astype(jnp.float32))
        delta_one = grouped_three(triple_low, inward, N_TENSOR)
        in_rows = delta_resid + norm_backward(delta_one, unit_one, scale_one, vecf[0])
        grad_rows_vec = jnp.stack([lax.optimization_barrier(jnp.sum(delta_one * unit_one, axis=0)), lax.optimization_barrier(jnp.sum(delta_one, axis=0)), lax.optimization_barrier(jnp.sum(delta_two * unit_two, axis=0)), lax.optimization_barrier(jnp.sum(delta_two, axis=0)), lax.optimization_barrier(jnp.sum(delta_resid, axis=0)), lax.optimization_barrier(jnp.sum(grad_flat, axis=0))])
        terms = (grad_inward, grad_outward, grad_widen, grad_narrow, grad_heads, grad_hidden, grad_rows_vec)
        carry = tuple((total + term for total, term in zip(carry, terms)))
        return (carry, (out_rows.reshape(SLOTS, SEQ, D), in_rows.reshape(SLOTS, SEQ, D)))
    start = (jnp.zeros((D, 3, D), jnp.float32), jnp.zeros((D, D), jnp.float32), jnp.zeros((D, FF), jnp.float32), jnp.zeros((FF, D), jnp.float32), jnp.zeros((2, D), jnp.float32), jnp.zeros((FF,), jnp.float32), jnp.zeros((6, D), jnp.float32))
    inputs = (block_input.reshape(N_FSDP, SLOTS, SEQ, D), output_grad.reshape(N_FSDP, SLOTS, SEQ, D), live_images.reshape(N_FSDP, SLOTS))
    totals, (outputs, in_grads) = lax.scan(one_block, start, inputs)
    block_output = outputs.reshape(IMAGES, SEQ, D)
    input_grad = in_grads.reshape(IMAGES, SEQ, D)
    grad_qkv, grad_out, grad_fc1, grad_fc2, grad_qvb, grad_fc1b, grad_vec = totals
    grad_qvb = grad_qvb.reshape(2, HEADS, HD)
    grad_fc1b = grad_fc1b.reshape(FF // HD, HD)
    params = (w_qkv, w_out, w_fc1, w_fc2, qv_bias, fc1_bias, norm_vec)
    grads = (grad_qkv, grad_out, grad_fc1, grad_fc2, grad_qvb, grad_fc1b, grad_vec)
    moments = (mom_qkv, mom_out, mom_fc1, mom_fc2, mom_qvb, mom_fc1b, mom_vec)
    stepped = [adamw(param, grad, moment) for param, grad, moment in zip(params, grads, moments)]
    return (block_output, input_grad, grad_qkv, grad_out, grad_fc1, grad_fc2, grad_qvb, grad_fc1b, grad_vec, stepped[0][0], stepped[1][0], stepped[2][0], stepped[3][0], stepped[4][0], stepped[5][0], stepped[6][0], stepped[0][1], stepped[1][1], stepped[2][1], stepped[3][1], stepped[4][1], stepped[5][1], stepped[6][1])
```

```python
import functools

import jax
import jax.numpy as jnp
from jax import lax
from jax.experimental import pallas as pl
from jax.experimental.pallas import tpu as pltpu
from jax.sharding import PartitionSpec as P

HD = 64


epsilon = 1e-06
sqrt_half = 0.7071067811865476
inv_root = 0.3989422804014327
corr_one = 1.0 - 0.9**3
corr_two = 1.0 - 0.999**3


def norm_forward(values, gain, shift):
    center = values - jnp.mean(values, axis=-1, keepdims=True)
    variance = jnp.mean(center * center, axis=-1, keepdims=True)
    scale = lax.rsqrt(variance + epsilon)
    normed = center * scale
    return (normed * gain + shift, normed, scale)


def norm_backward(upstream, normed, scale, gain):
    scaled = upstream * gain
    return scale * (
        scaled
        - jnp.mean(scaled, axis=-1, keepdims=True)
        - normed * jnp.mean(scaled * normed, axis=-1, keepdims=True)
    )


def gelu_slope(pre_act):
    return (
        0.5 * (1.0 + lax.erf(pre_act * sqrt_half))
        + pre_act * jnp.exp(-0.5 * pre_act * pre_act) * inv_root
    )


def attend(queries, key_rows, value_rows):
    scores = (
        jnp.einsum("bqhe,bkhe->bhqk", queries, key_rows, preferred_element_type=jnp.float32) * 0.125
    )
    logsum = jax.nn.logsumexp(scores, axis=-1, keepdims=True)
    probs = jnp.exp(scores - logsum).astype(jnp.bfloat16)
    mixed = jnp.einsum("bhqk,bkhe->bqhe", probs, value_rows, preferred_element_type=jnp.float32)
    return (mixed.astype(jnp.bfloat16), logsum)


def attend_back(queries, key_rows, value_rows, logsum, upstream):
    scores = (
        jnp.einsum("bqhe,bkhe->bhqk", queries, key_rows, preferred_element_type=jnp.float32) * 0.125
    )
    probs = jnp.exp(scores - logsum)
    probs_low = probs.astype(jnp.bfloat16)
    dprobs = jnp.einsum("bqhe,bkhe->bhqk", upstream, value_rows, preferred_element_type=jnp.float32)
    dscore = (probs * (dprobs - jnp.sum(probs * dprobs, axis=-1, keepdims=True))).astype(
        jnp.bfloat16
    )
    dquery = 0.125 * jnp.einsum(
        "bhqk,bkhe->bqhe", dscore, key_rows, preferred_element_type=jnp.float32
    )
    dkey = 0.125 * jnp.einsum(
        "bhqk,bqhe->bkhe", dscore, queries, preferred_element_type=jnp.float32
    )
    dvalue = jnp.einsum("bhqk,bqhe->bkhe", probs_low, upstream, preferred_element_type=jnp.float32)
    return (dquery, dkey, dvalue)


def adamw(param, grad, moments):
    first = 0.9 * moments[0] + 0.1 * grad
    second = 0.999 * moments[1] + 0.001 * grad * grad
    fresh = param - 0.004 * (
        first / corr_one / (jnp.sqrt(second / corr_two) + 1e-08) + 0.05 * param
    )
    return (fresh, jnp.stack([first, second]))


MESH_ID = pl.DeviceIdType.MESH


def exchange(fsdp, tensor, tag, gathers=(), reduces=(), terms=()):
    far_n, across_n = fsdp // 2, tensor // 2
    n_g, n_r, n_t = len(gathers), len(reduces), len(terms)
    low = jnp.bfloat16

    def kernel(*refs):
        refs = list(refs)

        def take(count):
            out, refs[:] = refs[:count], refs[count:]
            return out

        g_in, r_in, t_in = take(n_g), take(n_r), take(n_t)
        g_out, r_out, t_out = take(n_g), take(n_r), take(n_t)
        r_near, r_sum, r_far = take(n_r), take(n_r), take(n_r)
        t_core, t_half, t_across = take(n_t), take(n_t), take(n_t)
        g_send, g_recv, r_send, r_recv, t_send, t_recv = take(6)
        mine = lax.axis_index("fsdp")
        lane = lax.axis_index("tensor")
        far, near = lax.div(mine, 2), lax.rem(mine, 2)
        across, core = lax.div(lane, 2), lax.rem(lane, 2)
        twin = 2 * far + (1 - near)
        mate = 2 * across + (1 - core)

        def ahead(step):
            return lax.rem(far + step, far_n)

        def behind(step):
            return lax.rem(far + far_n - step, far_n)

        barrier = pltpu.get_barrier_semaphore()
        greeted = 0
        if n_g or n_r:
            for who in [twin] + [2 * ahead(j) + near for j in range(1, far_n)]:
                pl.semaphore_signal(barrier, inc=1, device_id=(who, lane), device_id_type=MESH_ID)
                greeted += 1
        if n_t:
            for who in [mate] + [
                2 * lax.rem(across + j, across_n) + core for j in range(1, across_n)
            ]:
                pl.semaphore_signal(barrier, inc=1, device_id=(mine, who), device_id_type=MESH_ID)
                greeted += 1
        pl.semaphore_wait(barrier, greeted)

        def copy(src, dst, send, recv, target):
            return pltpu.make_async_remote_copy(
                src_ref=src,
                dst_ref=dst,
                send_sem=send,
                recv_sem=recv,
                device_id=target,
                device_id_type=MESH_ID,
            )

        def run_gather():
            sent = []
            for j in range(1, far_n):
                for p in range(n_g):
                    sent.append(
                        copy(g_in[p], g_out[p].at[mine], g_send.at[p, j], g_recv.at[p, j],
                             (2 * ahead(j) + near, lane))
                    )
                    sent[-1].start()
            for p in range(n_g):
                sent.append(
                    copy(g_in[p], g_out[p].at[mine], g_send.at[p, far_n], g_recv.at[p, far_n],
                         (twin, lane))
                )
                sent[-1].start()
                g_out[p][mine] = g_in[p][...]
            yield
            for j in range(1, far_n):
                for p in range(n_g):
                    slot = g_out[p].at[2 * behind(j) + near]
                    copy(g_in[p], slot, g_send.at[p, j], g_recv.at[p, j],
                         (2 * ahead(j) + near, lane)).wait_recv()
                    sent.append(
                        copy(slot, slot, g_send.at[p, far_n + j], g_recv.at[p, far_n + j],
                             (twin, lane))
                    )
                    sent[-1].start()
                yield
            for j in range(far_n):
                for p in range(n_g):
                    slot = g_out[p].at[2 * behind(j) + (1 - near)]
                    copy(g_in[p], slot, g_send.at[p, far_n + j], g_recv.at[p, far_n + j],
                         (twin, lane)).wait_recv()
            for entry in sent:
                entry.wait_send()

        def run_reduce():
            order = list(range(1, far_n)) + [0]
            hops = {}
            for p in range(n_r):
                for j in order:
                    hops[p, j] = copy(
                        r_in[p].at[2 * ahead(j) + (1 - near)], r_near[p].at[j],
                        r_send.at[p, j], r_recv.at[p, j], (twin, lane))
                    hops[p, j].start()
            yield
            sent = {}
            for p in range(n_r):
                for j in range(1, far_n):
                    hops[p, j].wait_recv()
                    total = r_in[p][2 * ahead(j) + near].astype(jnp.float32) + r_near[p][j].astype(
                        jnp.float32
                    )
                    r_sum[p][j - 1] = total.astype(r_sum[p].dtype)
                    sent[p, j] = copy(
                        r_sum[p].at[j - 1], r_far[p].at[j - 1],
                        r_send.at[p, far_n + j], r_recv.at[p, far_n + j],
                        (2 * ahead(j) + near, lane))
                    sent[p, j].start()
                    yield
            for p in range(n_r):
                hops[p, 0].wait_recv()
                total = r_in[p][mine].astype(jnp.float32) + r_near[p][0].astype(jnp.float32)
                for j in range(1, far_n):
                    sent[p, j].wait_recv()
                    total = total + r_far[p][j - 1].astype(jnp.float32)
                r_out[p][...] = total
            for entry in list(hops.values()) + list(sent.values()):
                entry.wait_send()

        def run_terms():
            half = [ref.shape[1] // 2 for ref in t_in]
            own = [pl.ds(pl.multiple_of(core * h, h), h) for h in half]
            other = [pl.ds(pl.multiple_of((1 - core) * h, h), h) for h in half]
            first, second, third = {}, {}, {}
            for p in range(n_t):
                first[p] = copy(t_in[p].at[:, other[p]], t_core[p], t_send.at[p, 0],
                                t_recv.at[p, 0], (mine, mate))
                first[p].start()
            yield
            for p in range(n_t):
                first[p].wait_recv()
                t_half[p][...] = (
                    t_in[p][:, own[p]].astype(jnp.float32) + t_core[p][...].astype(jnp.float32)
                ).astype(low)
                for j in range(1, across_n):
                    second[p, j] = copy(
                        t_half[p], t_across[p].at[j - 1], t_send.at[p, 1 + j], t_recv.at[p, 1 + j],
                        (mine, 2 * lax.rem(across + j, across_n) + core))
                    second[p, j].start()
            yield
            yield
            for p in range(n_t):
                total = t_half[p][...].astype(jnp.float32)
                for j in range(1, across_n):
                    second[p, j].wait_recv()
                    total = total + t_across[p][j - 1].astype(jnp.float32)
                t_out[p][:, own[p]] = total.astype(low)
                third[p] = copy(t_out[p].at[:, own[p]], t_out[p].at[:, own[p]], t_send.at[p, 1],
                                t_recv.at[p, 1], (mine, mate))
                third[p].start()
            yield
            for p in range(n_t):
                copy(t_out[p].at[:, own[p]], t_out[p].at[:, other[p]], t_send.at[p, 1],
                     t_recv.at[p, 1], (mine, mate)).wait_recv()
            for entry in list(first.values()) + list(second.values()) + list(third.values()):
                entry.wait_send()

        flows = []
        if n_t:
            flows.append(run_terms())
        if n_g:
            flows.append(run_gather())
        if n_r:
            flows.append(run_reduce())
        while flows:
            for flow in list(flows):
                if next(flow, "end") == "end":
                    flows.remove(flow)

    shape = jax.ShapeDtypeStruct
    outs = (
        [shape((fsdp,) + a.shape, a.dtype) for a in gathers]
        + [shape(a.shape[1:], jnp.float32) for a in reduces]
        + [shape(a.shape, a.dtype) for a in terms]
    )
    few = max(far_n - 1, 1)
    scratch = (
        [pltpu.VMEM((far_n,) + a.shape[1:], a.dtype) for a in reduces]
        + [pltpu.VMEM((few,) + a.shape[1:], a.dtype) for a in reduces]
        + [pltpu.VMEM((few,) + a.shape[1:], a.dtype) for a in reduces]
        + [pltpu.VMEM((a.shape[0], a.shape[1] // 2), low) for a in terms]
        + [pltpu.VMEM((a.shape[0], a.shape[1] // 2), low) for a in terms]
        + [pltpu.VMEM((max(across_n - 1, 1), a.shape[0], a.shape[1] // 2), low) for a in terms]
        + [pltpu.SemaphoreType.DMA((max(n_g, 1), 2 * far_n))] * 2
        + [pltpu.SemaphoreType.DMA((max(n_r, 1), 2 * far_n))] * 2
        + [pltpu.SemaphoreType.DMA((max(n_t, 1), 1 + across_n))] * 2
    )
    args = tuple(gathers) + tuple(reduces) + tuple(terms)
    return pl.pallas_call(
        kernel,
        out_shape=tuple(outs),
        in_specs=[pl.BlockSpec(memory_space=pltpu.VMEM)] * len(args),
        out_specs=tuple([pl.BlockSpec(memory_space=pltpu.VMEM)] * len(outs)),
        scratch_shapes=scratch,
        compiler_params=pltpu.CompilerParams(
            collective_id=tag, has_side_effects=True, vmem_limit_bytes=48 * 1024 * 1024
        ),
        name="exchange_" + str(tag),
    )(*args)


def row_of(values, lanes):
    return jnp.pad(values, [(0, 0)] * (values.ndim - 1) + [(0, lanes - values.shape[-1])])


def on_device(
    fsdp,
    tensor,
    block_input,
    output_grad,
    live_images,
    w_qkv,
    w_out,
    w_fc1,
    w_fc2,
    qv_bias,
    fc1_bias,
    norm_vec,
    mom_qkv,
    mom_out,
    mom_fc1,
    mom_fc2,
    mom_qvb,
    mom_fc1b,
    mom_vec,
):
    low = jnp.bfloat16
    images, seqlen, width = block_input.shape
    rows = images * seqlen
    owned_rows, _, local_feat = w_qkv.shape
    hidden = w_fc1.shape[1]
    heads_here = local_feat // HD
    n_qvb, n_fc1b = qv_bias.size, fc1_bias.size
    vec_rows = norm_vec.shape[0]
    lanes = -(-max(owned_rows, n_qvb, n_fc1b) // 128) * 128
    small_rows = 16

    small = jnp.concatenate(
        [
            row_of(norm_vec, lanes),
            row_of(fc1_bias.reshape(1, n_fc1b), lanes),
            row_of(qv_bias.reshape(1, n_qvb), lanes),
            jnp.zeros((small_rows - vec_rows - 2, lanes), jnp.float32),
        ]
    ).astype(low)
    small_all, inward, outward = exchange(
        fsdp,
        tensor,
        1,
        gathers=(
            small,
            w_qkv.astype(low).reshape(owned_rows, 3 * local_feat),
            w_out.astype(low).T,
        ),
    )
    inward = inward.reshape(width, 3 * local_feat)
    outward = outward.reshape(width, local_feat)
    smallf = small_all.astype(jnp.float32)
    vecf = smallf[:, :vec_rows, :owned_rows].transpose(1, 0, 2).reshape(vec_rows, width)
    hidden_bias = (
        smallf[:, vec_rows, :n_fc1b]
        .reshape((fsdp,) + fc1_bias.shape)
        .transpose(1, 0, 2)
        .reshape(hidden)
    )
    biasf = (
        smallf[:, vec_rows + 1, :n_qvb]
        .reshape((fsdp,) + qv_bias.shape)
        .transpose(1, 2, 0, 3)
        .reshape(2, local_feat)
    )
    flat = block_input.astype(jnp.float32).reshape(rows, width)
    first_norm, unit_one, scale_one = norm_forward(flat, vecf[0], vecf[1])
    normed_one = first_norm.astype(low)
    shifts = jnp.concatenate([biasf[0], jnp.zeros_like(biasf[0]), biasf[1]])
    projected = jnp.dot(normed_one, inward, preferred_element_type=jnp.float32) + shifts
    triple = projected.astype(low).reshape(images, seqlen, 3, heads_here, HD)
    queries = triple[:, :, 0]
    key_rows = triple[:, :, 1]
    value_rows = triple[:, :, 2]
    mixed, logsum = attend(queries, key_rows, value_rows)
    attn_rows = mixed.reshape(rows, local_feat)
    attn_term = jnp.einsum(
        "nj,dj->nd", attn_rows, outward, preferred_element_type=jnp.float32
    ).astype(low)
    widen, narrow, attn_total = exchange(
        fsdp,
        tensor,
        2,
        gathers=(w_fc1.astype(low), w_fc2.astype(low).T),
        terms=(attn_term,),
    )
    widen = widen.reshape(width, hidden)
    narrow = narrow.reshape(width, hidden)
    resid = flat + attn_total.astype(jnp.float32) + vecf[4]
    second_norm, unit_two, scale_two = norm_forward(resid, vecf[2], vecf[3])
    normed_two = second_norm.astype(low)
    pre_act = jnp.dot(normed_two, widen, preferred_element_type=jnp.float32) + hidden_bias
    activ = jax.nn.gelu(pre_act, approximate=False).astype(low)
    mlp_term = jnp.einsum(
        "nf,df->nd", activ, narrow, preferred_element_type=jnp.float32
    ).astype(low)
    row_mask = jnp.broadcast_to(live_images.astype(jnp.float32)[:, None], (images, seqlen)).reshape(
        rows, 1
    )
    grad_flat = output_grad.astype(jnp.float32).reshape(rows, width) * row_mask
    grad_low = grad_flat.astype(low)
    grad_narrow = jnp.einsum("nd,nf->df", grad_low, activ, preferred_element_type=jnp.float32)
    delta_act = jnp.einsum("nd,df->nf", grad_low, narrow, preferred_element_type=jnp.float32)
    delta_pre = delta_act * gelu_slope(pre_act)
    delta_pre_low = delta_pre.astype(low)
    grad_hidden = jnp.sum(delta_pre, axis=0)
    grad_widen = jnp.einsum(
        "nd,nf->df", normed_two, delta_pre_low, preferred_element_type=jnp.float32
    )
    two_term = jnp.einsum(
        "nf,df->nd", delta_pre_low, widen, preferred_element_type=jnp.float32
    ).astype(low)

    def blocks(grad):
        return grad.astype(low).reshape(fsdp, owned_rows, grad.shape[1])

    own_narrow, own_widen, delta_two, mlp_total = exchange(
        fsdp,
        tensor,
        3,
        reduces=(blocks(grad_narrow), blocks(grad_widen)),
        terms=(two_term, mlp_term),
    )
    delta_two = delta_two.astype(jnp.float32)
    block_output = (
        (row_mask * (resid + mlp_total.astype(jnp.float32) + vecf[5]))
        .astype(low)
        .reshape(images, seqlen, width)
    )
    delta_resid = grad_flat + norm_backward(delta_two, unit_two, scale_two, vecf[2])
    delta_resid_low = delta_resid.astype(low)
    grad_outward = jnp.einsum(
        "nd,nj->dj", delta_resid_low, attn_rows, preferred_element_type=jnp.float32
    )
    delta_mixed = jnp.dot(delta_resid_low, outward, preferred_element_type=jnp.float32)
    delta_mixed = delta_mixed.astype(low).reshape(images, seqlen, heads_here, HD)
    delta_query, delta_key, delta_value = attend_back(
        queries, key_rows, value_rows, logsum, delta_mixed
    )
    delta_triple = jnp.stack([delta_query, delta_key, delta_value], axis=2).reshape(
        rows, 3 * local_feat
    )
    grad_heads = jnp.stack(
        [
            jnp.sum(delta_query, axis=(0, 1)).reshape(local_feat),
            jnp.sum(delta_value, axis=(0, 1)).reshape(local_feat),
        ]
    )
    triple_low = delta_triple.astype(low)
    grad_inward = jnp.einsum(
        "nd,nj->dj", normed_one, triple_low, preferred_element_type=jnp.float32
    )
    one_term = jnp.einsum(
        "nj,dj->nd", triple_low, inward, preferred_element_type=jnp.float32
    ).astype(low)
    own_inward, own_outward, delta_one = exchange(
        fsdp,
        tensor,
        4,
        reduces=(blocks(grad_inward), blocks(grad_outward)),
        terms=(one_term,),
    )
    delta_one = delta_one.astype(jnp.float32)
    input_grad = (delta_resid + norm_backward(delta_one, unit_one, scale_one, vecf[0])).reshape(
        images, seqlen, width
    )
    grad_rows_vec = jnp.stack(
        [
            jnp.sum(delta_one * unit_one, axis=0),
            jnp.sum(delta_one, axis=0),
            jnp.sum(delta_two * unit_two, axis=0),
            jnp.sum(delta_two, axis=0),
            jnp.sum(delta_resid, axis=0),
            jnp.sum(grad_flat, axis=0),
        ]
    )
    r_fc1b, c_fc1b = fc1_bias.shape
    k_qvb, r_qvb, c_qvb = qv_bias.shape
    small_grads = jnp.concatenate(
        [
            row_of(grad_rows_vec.reshape(vec_rows, fsdp, owned_rows).transpose(1, 0, 2), lanes),
            row_of(
                grad_hidden.reshape(r_fc1b, fsdp, c_fc1b).transpose(1, 0, 2).reshape(
                    fsdp, 1, n_fc1b
                ),
                lanes,
            ),
            row_of(
                grad_heads.reshape(k_qvb, r_qvb, fsdp, c_qvb).transpose(2, 0, 1, 3).reshape(
                    fsdp, 1, n_qvb
                ),
                lanes,
            ),
        ],
        axis=1,
    )
    (own_small,) = exchange(fsdp, tensor, 5, reduces=(small_grads,))
    owned = (
        own_inward.reshape(w_qkv.shape),
        own_outward.T,
        own_widen,
        own_narrow.T,
        own_small[vec_rows + 1, :n_qvb].reshape(qv_bias.shape),
        own_small[vec_rows, :n_fc1b].reshape(fc1_bias.shape),
        own_small[:vec_rows, :owned_rows],
    )
    params = (w_qkv, w_out, w_fc1, w_fc2, qv_bias, fc1_bias, norm_vec)
    moments = (mom_qkv, mom_out, mom_fc1, mom_fc2, mom_qvb, mom_fc1b, mom_vec)
    stepped = [adamw(param, grad, moment) for param, grad, moment in zip(params, owned, moments)]
    return (
        (block_output, input_grad)
        + tuple(owned)
        + tuple((entry[0] for entry in stepped))
        + tuple((entry[1] for entry in stepped))
    )


def solution(mesh):
    return jax.shard_map(
        functools.partial(on_device, mesh.shape["fsdp"], mesh.shape["tensor"]),
        mesh=mesh,
        in_specs=(
            P("fsdp", None, None),
            P("fsdp", None, None),
            P("fsdp"),
            P("fsdp", None, "tensor"),
            P("tensor", "fsdp"),
            P("fsdp", "tensor"),
            P("tensor", "fsdp"),
            P(None, "tensor", "fsdp"),
            P("tensor", "fsdp"),
            P(None, "fsdp"),
            P(None, "fsdp", None, "tensor"),
            P(None, "tensor", "fsdp"),
            P(None, "fsdp", "tensor"),
            P(None, "tensor", "fsdp"),
            P(None, None, "tensor", "fsdp"),
            P(None, "tensor", "fsdp"),
            P(None, None, "fsdp"),
        ),
        out_specs=(
            P("fsdp", None, None),
            P("fsdp", None, None),
            P("fsdp", None, "tensor"),
            P("tensor", "fsdp"),
            P("fsdp", "tensor"),
            P("tensor", "fsdp"),
            P(None, "tensor", "fsdp"),
            P("tensor", "fsdp"),
            P(None, "fsdp"),
            P("fsdp", None, "tensor"),
            P("tensor", "fsdp"),
            P("fsdp", "tensor"),
            P("tensor", "fsdp"),
            P(None, "tensor", "fsdp"),
            P("tensor", "fsdp"),
            P(None, "fsdp"),
            P(None, "fsdp", None, "tensor"),
            P(None, "tensor", "fsdp"),
            P(None, "fsdp", "tensor"),
            P(None, "tensor", "fsdp"),
            P(None, None, "tensor", "fsdp"),
            P(None, "tensor", "fsdp"),
            P(None, None, "fsdp"),
        ),
        check_vma=False,
    )
```

```python
import functools

import jax
import jax.numpy as jnp
from jax import lax
from jax.experimental import pallas as pl
from jax.experimental.pallas import tpu as pltpu
from jax.sharding import PartitionSpec as P

HD = 64


epsilon = 1e-06
sqrt_half = 0.7071067811865476
inv_root = 0.3989422804014327
corr_one = 1.0 - 0.9**3
corr_two = 1.0 - 0.999**3


def norm_forward(values, gain, shift):
    center = values - jnp.mean(values, axis=-1, keepdims=True)
    variance = jnp.mean(center * center, axis=-1, keepdims=True)
    scale = lax.rsqrt(variance + epsilon)
    normed = center * scale
    return (normed * gain + shift, normed, scale)


def norm_backward(upstream, normed, scale, gain):
    scaled = upstream * gain
    return scale * (
        scaled
        - jnp.mean(scaled, axis=-1, keepdims=True)
        - normed * jnp.mean(scaled * normed, axis=-1, keepdims=True)
    )


def gelu_slope(pre_act):
    return (
        0.5 * (1.0 + lax.erf(pre_act * sqrt_half))
        + pre_act * jnp.exp(-0.5 * pre_act * pre_act) * inv_root
    )


def attend(queries, key_rows, value_rows):
    scores = (
        jnp.einsum("bqhe,bkhe->bhqk", queries, key_rows, preferred_element_type=jnp.float32) * 0.125
    )
    logsum = jax.nn.logsumexp(scores, axis=-1, keepdims=True)
    probs = jnp.exp(scores - logsum).astype(jnp.bfloat16)
    mixed = jnp.einsum("bhqk,bkhe->bqhe", probs, value_rows, preferred_element_type=jnp.float32)
    return (mixed.astype(jnp.bfloat16), logsum)


def attend_back(queries, key_rows, value_rows, logsum, upstream):
    scores = (
        jnp.einsum("bqhe,bkhe->bhqk", queries, key_rows, preferred_element_type=jnp.float32) * 0.125
    )
    probs = jnp.exp(scores - logsum)
    probs_low = probs.astype(jnp.bfloat16)
    dprobs = jnp.einsum("bqhe,bkhe->bhqk", upstream, value_rows, preferred_element_type=jnp.float32)
    dscore = (probs * (dprobs - jnp.sum(probs * dprobs, axis=-1, keepdims=True))).astype(
        jnp.bfloat16
    )
    dquery = 0.125 * jnp.einsum(
        "bhqk,bkhe->bqhe", dscore, key_rows, preferred_element_type=jnp.float32
    )
    dkey = 0.125 * jnp.einsum(
        "bhqk,bqhe->bkhe", dscore, queries, preferred_element_type=jnp.float32
    )
    dvalue = jnp.einsum("bhqk,bqhe->bkhe", probs_low, upstream, preferred_element_type=jnp.float32)
    return (dquery, dkey, dvalue)


def adamw(param, grad, moments):
    first = 0.9 * moments[0] + 0.1 * grad
    second = 0.999 * moments[1] + 0.001 * grad * grad
    fresh = param - 0.004 * (
        first / corr_one / (jnp.sqrt(second / corr_two) + 1e-08) + 0.05 * param
    )
    return (fresh, jnp.stack([first, second]))


MESH_ID = pl.DeviceIdType.MESH


def exchange(fsdp, tensor, tag, gathers=(), reduces=(), terms=(), shared_rows=0):
    far_n, across_n = fsdp // 2, tensor // 2
    n_g, n_r, n_t = len(gathers), len(reduces), len(terms)
    low = jnp.bfloat16

    def kernel(*refs):
        refs = list(refs)

        def take(count):
            out, refs[:] = refs[:count], refs[count:]
            return out

        g_in, r_in, t_in = take(n_g), take(n_r), take(n_t)
        g_out, r_out, t_out = take(n_g), take(n_r), take(n_t)
        r_near, r_sum, r_far = take(n_r), take(n_r), take(n_r)
        t_core, t_half, t_across = take(n_t), take(n_t), take(n_t)
        peers, p_send, p_recv = take(3) if shared_rows else (None, None, None)
        g_send, g_recv, r_send, r_recv, t_send, t_recv = take(6)
        mine = lax.axis_index("fsdp")
        lane = lax.axis_index("tensor")
        far, near = lax.div(mine, 2), lax.rem(mine, 2)
        across, core = lax.div(lane, 2), lax.rem(lane, 2)
        twin = 2 * far + (1 - near)
        mate = 2 * across + (1 - core)

        def ahead(step):
            return lax.rem(far + step, far_n)

        def behind(step):
            return lax.rem(far + far_n - step, far_n)

        barrier = pltpu.get_barrier_semaphore()
        greeted = 0
        if n_g or n_r:
            for who in [twin] + [2 * ahead(j) + near for j in range(1, far_n)]:
                pl.semaphore_signal(barrier, inc=1, device_id=(who, lane), device_id_type=MESH_ID)
                greeted += 1
        if n_t:
            whom = [mate] + [2 * lax.rem(across + j, across_n) + core for j in range(1, across_n)]
            if shared_rows:
                whom = [lax.rem(lane + j, tensor) for j in range(1, tensor)]
            for who in whom:
                pl.semaphore_signal(barrier, inc=1, device_id=(mine, who), device_id_type=MESH_ID)
                greeted += 1
        pl.semaphore_wait(barrier, greeted)

        def copy(src, dst, send, recv, target):
            return pltpu.make_async_remote_copy(
                src_ref=src,
                dst_ref=dst,
                send_sem=send,
                recv_sem=recv,
                device_id=target,
                device_id_type=MESH_ID,
            )

        def run_gather():
            sent = []
            for j in range(1, far_n):
                for p in range(n_g):
                    sent.append(
                        copy(g_in[p], g_out[p].at[mine], g_send.at[p, j], g_recv.at[p, j],
                             (2 * ahead(j) + near, lane))
                    )
                    sent[-1].start()
            for p in range(n_g):
                sent.append(
                    copy(g_in[p], g_out[p].at[mine], g_send.at[p, far_n], g_recv.at[p, far_n],
                         (twin, lane))
                )
                sent[-1].start()
                g_out[p][mine] = g_in[p][...]
            yield
            for j in range(1, far_n):
                for p in range(n_g):
                    slot = g_out[p].at[2 * behind(j) + near]
                    copy(g_in[p], slot, g_send.at[p, j], g_recv.at[p, j],
                         (2 * ahead(j) + near, lane)).wait_recv()
                    sent.append(
                        copy(slot, slot, g_send.at[p, far_n + j], g_recv.at[p, far_n + j],
                             (twin, lane))
                    )
                    sent[-1].start()
                yield
            for j in range(far_n):
                for p in range(n_g):
                    slot = g_out[p].at[2 * behind(j) + (1 - near)]
                    copy(g_in[p], slot, g_send.at[p, far_n + j], g_recv.at[p, far_n + j],
                         (twin, lane)).wait_recv()
            for entry in sent:
                entry.wait_send()

        def run_reduce():
            order = list(range(1, far_n)) + [0]
            hops = {}
            for p in range(n_r):
                for j in order:
                    hops[p, j] = copy(
                        r_in[p].at[2 * ahead(j) + (1 - near)], r_near[p].at[j],
                        r_send.at[p, j], r_recv.at[p, j], (twin, lane))
                    hops[p, j].start()
            yield
            sent = {}
            for p in range(n_r):
                for j in range(1, far_n):
                    hops[p, j].wait_recv()
                    total = r_in[p][2 * ahead(j) + near].astype(jnp.float32) + r_near[p][j].astype(
                        jnp.float32
                    )
                    r_sum[p][j - 1] = total.astype(r_sum[p].dtype)
                    sent[p, j] = copy(
                        r_sum[p].at[j - 1], r_far[p].at[j - 1],
                        r_send.at[p, far_n + j], r_recv.at[p, far_n + j],
                        (2 * ahead(j) + near, lane))
                    sent[p, j].start()
                    yield
            shared = []
            for p in range(n_r):
                hops[p, 0].wait_recv()
                total = r_in[p][mine].astype(jnp.float32) + r_near[p][0].astype(jnp.float32)
                for j in range(1, far_n):
                    sent[p, j].wait_recv()
                    total = total + r_far[p][j - 1].astype(jnp.float32)
                if p == 0 and shared_rows:
                    peers[lane] = total
                    for j in range(1, tensor):
                        shared.append(
                            copy(peers.at[lane], peers.at[lane], p_send.at[j], p_recv.at[j],
                                 (mine, lax.rem(lane + j, tensor))))
                        shared[-1].start()
                    yield
                r_out[p][...] = total
            for j in range(1, tensor if shared_rows else 1):
                source = peers.at[lax.rem(lane + tensor - j, tensor)]
                copy(source, source, p_send.at[j], p_recv.at[j],
                     (mine, lax.rem(lane + j, tensor))).wait_recv()
            if shared_rows:
                total = peers[0]
                for j in range(1, tensor):
                    total = total + peers[j]
                which = lax.broadcasted_iota(jnp.int32, total.shape, 0)
                r_out[0][...] = jnp.where(which < shared_rows, total, r_out[0][...])
            for entry in shared:
                entry.wait_send()
            for entry in list(hops.values()) + list(sent.values()):
                entry.wait_send()

        def run_terms():
            half = [ref.shape[1] // 2 for ref in t_in]
            own = [pl.ds(pl.multiple_of(core * h, h), h) for h in half]
            other = [pl.ds(pl.multiple_of((1 - core) * h, h), h) for h in half]
            first, second, third = {}, {}, {}
            for p in range(n_t):
                first[p] = copy(t_in[p].at[:, other[p]], t_core[p], t_send.at[p, 0],
                                t_recv.at[p, 0], (mine, mate))
                first[p].start()
            yield
            for p in range(n_t):
                first[p].wait_recv()
                t_half[p][...] = (
                    t_in[p][:, own[p]].astype(jnp.float32) + t_core[p][...].astype(jnp.float32)
                ).astype(low)
                for j in range(1, across_n):
                    second[p, j] = copy(
                        t_half[p], t_across[p].at[j - 1], t_send.at[p, 1 + j], t_recv.at[p, 1 + j],
                        (mine, 2 * lax.rem(across + j, across_n) + core))
                    second[p, j].start()
            for _ in range(5 if n_t > 1 else 2):
                yield
            for p in range(n_t):
                total = t_half[p][...].astype(jnp.float32)
                for j in range(1, across_n):
                    second[p, j].wait_recv()
                    total = total + t_across[p][j - 1].astype(jnp.float32)
                t_out[p][:, own[p]] = total.astype(low)
                third[p] = copy(t_out[p].at[:, own[p]], t_out[p].at[:, own[p]], t_send.at[p, 1],
                                t_recv.at[p, 1], (mine, mate))
                third[p].start()
            yield
            for p in range(n_t):
                copy(t_out[p].at[:, own[p]], t_out[p].at[:, other[p]], t_send.at[p, 1],
                     t_recv.at[p, 1], (mine, mate)).wait_recv()
            for entry in list(first.values()) + list(second.values()) + list(third.values()):
                entry.wait_send()

        flows = []
        if n_t:
            flows.append(run_terms())
        if n_g:
            flows.append(run_gather())
        if n_r:
            flows.append(run_reduce())
        while flows:
            for flow in list(flows):
                if next(flow, "end") == "end":
                    flows.remove(flow)

    shape = jax.ShapeDtypeStruct
    outs = (
        [shape((fsdp,) + a.shape, a.dtype) for a in gathers]
        + [shape(a.shape[1:], jnp.float32) for a in reduces]
        + [shape(a.shape, a.dtype) for a in terms]
    )
    few = max(far_n - 1, 1)
    scratch = (
        [pltpu.VMEM((far_n,) + a.shape[1:], a.dtype) for a in reduces]
        + [pltpu.VMEM((few,) + a.shape[1:], a.dtype) for a in reduces]
        + [pltpu.VMEM((few,) + a.shape[1:], a.dtype) for a in reduces]
        + [pltpu.VMEM((a.shape[0], a.shape[1] // 2), low) for a in terms]
        + [pltpu.VMEM((a.shape[0], a.shape[1] // 2), low) for a in terms]
        + [pltpu.VMEM((max(across_n - 1, 1), a.shape[0], a.shape[1] // 2), low) for a in terms]
        + (
            [pltpu.VMEM((tensor,) + reduces[0].shape[1:], jnp.float32)]
            + [pltpu.SemaphoreType.DMA((tensor,))] * 2
            if shared_rows
            else []
        )
        + [pltpu.SemaphoreType.DMA((max(n_g, 1), 2 * far_n))] * 2
        + [pltpu.SemaphoreType.DMA((max(n_r, 1), 2 * far_n))] * 2
        + [pltpu.SemaphoreType.DMA((max(n_t, 1), 1 + across_n))] * 2
    )
    args = tuple(gathers) + tuple(reduces) + tuple(terms)
    return pl.pallas_call(
        kernel,
        out_shape=tuple(outs),
        in_specs=[pl.BlockSpec(memory_space=pltpu.VMEM)] * len(args),
        out_specs=tuple([pl.BlockSpec(memory_space=pltpu.VMEM)] * len(outs)),
        scratch_shapes=scratch,
        compiler_params=pltpu.CompilerParams(
            collective_id=tag, has_side_effects=True, vmem_limit_bytes=48 * 1024 * 1024
        ),
        name="exchange_" + str(tag),
    )(*args)


def step_all(params, grads, moments):
    count = len(params)

    def kernel(*refs):
        for p in range(count):
            param, grad, moment, fresh, copied, moved = refs[p::count]
            given = grad[...]
            first = 0.9 * moment[0] + 0.1 * given
            second = 0.999 * moment[1] + 0.001 * given * given
            fresh[...] = param[...] - 0.004 * (
                first / corr_one / (jnp.sqrt(second / corr_two) + 1e-08) + 0.05 * param[...]
            )
            copied[...] = given
            moved[0] = first
            moved[1] = second

    args = tuple(params) + tuple(grads) + tuple(moments)
    spec = pl.BlockSpec(memory_space=pltpu.VMEM)
    outs = pl.pallas_call(
        kernel,
        out_shape=tuple(jax.ShapeDtypeStruct(a.shape, a.dtype) for a in args),
        in_specs=[spec] * len(args),
        out_specs=tuple([spec] * len(args)),
        compiler_params=pltpu.CompilerParams(vmem_limit_bytes=48 * 1024 * 1024),
        name="step_all",
    )(*args)
    return outs[:count], outs[count : 2 * count], outs[2 * count :]


def row_of(values, lanes):
    return jnp.pad(values, [(0, 0)] * (values.ndim - 1) + [(0, lanes - values.shape[-1])])


def on_device(
    fsdp,
    tensor,
    block_input,
    output_grad,
    live_images,
    w_qkv,
    w_out,
    w_fc1,
    w_fc2,
    qv_bias,
    fc1_bias,
    norm_vec,
    mom_qkv,
    mom_out,
    mom_fc1,
    mom_fc2,
    mom_qvb,
    mom_fc1b,
    mom_vec,
):
    low = jnp.bfloat16
    images, seqlen, width = block_input.shape
    rows = images * seqlen
    owned_rows, _, local_feat = w_qkv.shape
    hidden = w_fc1.shape[1]
    heads_here = local_feat // HD
    n_qvb, n_fc1b = qv_bias.size, fc1_bias.size
    vec_rows = norm_vec.shape[0]
    lanes = -(-max(owned_rows, n_qvb, n_fc1b) // 128) * 128
    small_rows = 16

    small = jnp.concatenate(
        [
            row_of(norm_vec, lanes),
            row_of(fc1_bias.reshape(1, n_fc1b), lanes),
            row_of(qv_bias.reshape(1, n_qvb), lanes),
            jnp.zeros((small_rows - vec_rows - 2, lanes), jnp.float32),
        ]
    ).astype(low)
    small_all, inward, outward = exchange(
        fsdp,
        tensor,
        1,
        gathers=(
            small,
            w_qkv.astype(low).reshape(owned_rows, 3 * local_feat),
            w_out.astype(low).T,
        ),
    )
    inward = inward.reshape(width, 3 * local_feat)
    outward = outward.reshape(width, local_feat)
    smallf = small_all.astype(jnp.float32)
    vecf = smallf[:, :vec_rows, :owned_rows].transpose(1, 0, 2).reshape(vec_rows, width)
    hidden_bias = (
        smallf[:, vec_rows, :n_fc1b]
        .reshape((fsdp,) + fc1_bias.shape)
        .transpose(1, 0, 2)
        .reshape(hidden)
    )
    biasf = (
        smallf[:, vec_rows + 1, :n_qvb]
        .reshape((fsdp,) + qv_bias.shape)
        .transpose(1, 2, 0, 3)
        .reshape(2, local_feat)
    )
    flat = block_input.transpose(1, 0, 2).reshape(rows, width).astype(jnp.float32)
    first_norm, unit_one, scale_one = norm_forward(flat, vecf[0], vecf[1])
    normed_one = first_norm.astype(low)
    shifts = jnp.concatenate([biasf[0], jnp.zeros_like(biasf[0]), biasf[1]])
    projected = jnp.dot(normed_one, inward, preferred_element_type=jnp.float32) + shifts
    triple = projected.astype(low).reshape(seqlen, images, 3, heads_here, HD)
    queries = triple[:, :, 0].transpose(1, 0, 2, 3)
    key_rows = triple[:, :, 1].transpose(1, 0, 2, 3)
    value_rows = triple[:, :, 2].transpose(1, 0, 2, 3)
    mixed, logsum = attend(queries, key_rows, value_rows)
    attn_rows = mixed.transpose(1, 0, 2, 3).reshape(rows, local_feat)
    attn_term = jnp.einsum(
        "nj,dj->nd", attn_rows, outward, preferred_element_type=jnp.float32
    ).astype(low)
    widen, narrow, attn_total = exchange(
        fsdp,
        tensor,
        2,
        gathers=(w_fc1.astype(low), w_fc2.astype(low).T),
        terms=(attn_term,),
    )
    widen = widen.reshape(width, hidden)
    narrow = narrow.reshape(width, hidden)
    resid = flat + attn_total.astype(jnp.float32) + vecf[4]
    second_norm, unit_two, scale_two = norm_forward(resid, vecf[2], vecf[3])
    normed_two = second_norm.astype(low)
    pre_act = jnp.dot(normed_two, widen, preferred_element_type=jnp.float32) + hidden_bias
    activ = jax.nn.gelu(pre_act, approximate=False).astype(low)
    mlp_term = jnp.einsum(
        "nf,df->nd", activ, narrow, preferred_element_type=jnp.float32
    ).astype(low)
    row_mask = jnp.broadcast_to(live_images.astype(jnp.float32)[None, :], (seqlen, images)).reshape(
        rows, 1
    )
    grad_flat = output_grad.transpose(1, 0, 2).reshape(rows, width).astype(jnp.float32) * row_mask
    grad_low = grad_flat.astype(low)
    grad_narrow = jnp.einsum("nd,nf->df", grad_low, activ, preferred_element_type=jnp.float32)
    delta_act = jnp.einsum("nd,df->nf", grad_low, narrow, preferred_element_type=jnp.float32)
    delta_pre = delta_act * gelu_slope(pre_act)
    delta_pre_low = delta_pre.astype(low)
    grad_hidden = jnp.sum(delta_pre, axis=0)
    grad_widen = jnp.einsum(
        "nd,nf->df", normed_two, delta_pre_low, preferred_element_type=jnp.float32
    )
    two_term = jnp.einsum(
        "nf,df->nd", delta_pre_low, widen, preferred_element_type=jnp.float32
    ).astype(low)

    def blocks(grad):
        return grad.astype(low).reshape(fsdp, owned_rows, grad.shape[1])

    own_narrow, own_widen, delta_two, mlp_total = exchange(
        fsdp,
        tensor,
        3,
        reduces=(blocks(grad_narrow), blocks(grad_widen)),
        terms=(two_term, mlp_term),
    )
    delta_two = delta_two.astype(jnp.float32)
    block_output = (
        (row_mask * (resid + mlp_total.astype(jnp.float32) + vecf[5]))
        .astype(low)
        .reshape(seqlen, images, width)
        .transpose(1, 0, 2)
    )
    delta_resid = grad_flat + norm_backward(delta_two, unit_two, scale_two, vecf[2])
    delta_resid_low = delta_resid.astype(low)
    grad_outward = jnp.einsum(
        "nd,nj->dj", delta_resid_low, attn_rows, preferred_element_type=jnp.float32
    )
    delta_mixed = jnp.dot(delta_resid_low, outward, preferred_element_type=jnp.float32)
    delta_mixed = (
        delta_mixed.astype(low).reshape(seqlen, images, heads_here, HD).transpose(1, 0, 2, 3)
    )
    delta_query, delta_key, delta_value = attend_back(
        queries, key_rows, value_rows, logsum, delta_mixed
    )
    delta_triple = jnp.concatenate(
        [
            part.transpose(1, 0, 2, 3).reshape(rows, local_feat)
            for part in (delta_query, delta_key, delta_value)
        ],
        axis=1,
    )
    grad_heads = jnp.stack(
        [
            jnp.sum(delta_query, axis=(0, 1)).reshape(local_feat),
            jnp.sum(delta_value, axis=(0, 1)).reshape(local_feat),
        ]
    )
    triple_low = delta_triple.astype(low)
    grad_inward = jnp.einsum(
        "nd,nj->dj", normed_one, triple_low, preferred_element_type=jnp.float32
    )
    one_term = jnp.einsum(
        "nj,dj->nd", triple_low, inward, preferred_element_type=jnp.float32
    ).astype(low)
    grad_rows_vec = jnp.stack(
        [
            jnp.sum(one_term.astype(jnp.float32) * unit_one, axis=0),
            jnp.sum(one_term.astype(jnp.float32), axis=0),
            jnp.sum(delta_two * unit_two, axis=0),
            jnp.sum(delta_two, axis=0),
            jnp.sum(delta_resid, axis=0),
            jnp.sum(grad_flat, axis=0),
        ]
    )
    r_fc1b, c_fc1b = fc1_bias.shape
    k_qvb, r_qvb, c_qvb = qv_bias.shape
    small_grads = jnp.concatenate(
        [
            row_of(grad_rows_vec.reshape(vec_rows, fsdp, owned_rows).transpose(1, 0, 2), lanes),
            row_of(
                grad_hidden.reshape(r_fc1b, fsdp, c_fc1b).transpose(1, 0, 2).reshape(
                    fsdp, 1, n_fc1b
                ),
                lanes,
            ),
            row_of(
                grad_heads.reshape(k_qvb, r_qvb, fsdp, c_qvb).transpose(2, 0, 1, 3).reshape(
                    fsdp, 1, n_qvb
                ),
                lanes,
            ),
            jnp.zeros((fsdp, small_rows - vec_rows - 2, lanes), jnp.float32),
        ],
        axis=1,
    )
    own_small, own_inward, own_outward, delta_one = exchange(
        fsdp,
        tensor,
        4,
        shared_rows=2,
        reduces=(small_grads, blocks(grad_inward), blocks(grad_outward)),
        terms=(one_term,),
    )
    delta_one = delta_one.astype(jnp.float32)
    input_grad = (delta_resid + norm_backward(delta_one, unit_one, scale_one, vecf[0])).reshape(
        seqlen, images, width
    ).transpose(1, 0, 2)
    fresh, given, moved = step_all(
        (w_qkv.transpose(1, 0, 2), w_out, w_fc1, w_fc2.T),
        (
            own_inward.reshape(w_qkv.shape).transpose(1, 0, 2),
            own_outward.T,
            own_widen,
            own_narrow,
        ),
        (
            mom_qkv.transpose(0, 2, 1, 3),
            mom_out,
            mom_fc1,
            mom_fc2.transpose(0, 2, 1),
        ),
    )
    small_owned = (
        own_small[vec_rows + 1, :n_qvb].reshape(qv_bias.shape),
        own_small[vec_rows, :n_fc1b].reshape(fc1_bias.shape),
        own_small[:vec_rows, :owned_rows],
    )
    stepped = [
        adamw(param, grad, moment)
        for param, grad, moment in zip(
            (qv_bias, fc1_bias, norm_vec), small_owned, (mom_qvb, mom_fc1b, mom_vec)
        )
    ]

    def placed(parts):
        return (parts[0].transpose(1, 0, 2), parts[1], parts[2], parts[3].T)

    return (
        (block_output, input_grad)
        + placed(given)
        + small_owned
        + placed(fresh)
        + tuple((entry[0] for entry in stepped))
        + (
            moved[0].transpose(0, 2, 1, 3),
            moved[1],
            moved[2],
            moved[3].transpose(0, 2, 1),
        )
        + tuple((entry[1] for entry in stepped))
    )


def solution(mesh):
    return jax.shard_map(
        functools.partial(on_device, mesh.shape["fsdp"], mesh.shape["tensor"]),
        mesh=mesh,
        in_specs=(
            P("fsdp", None, None),
            P("fsdp", None, None),
            P("fsdp"),
            P("fsdp", None, "tensor"),
            P("tensor", "fsdp"),
            P("fsdp", "tensor"),
            P("tensor", "fsdp"),
            P(None, "tensor", "fsdp"),
            P("tensor", "fsdp"),
            P(None, "fsdp"),
            P(None, "fsdp", None, "tensor"),
            P(None, "tensor", "fsdp"),
            P(None, "fsdp", "tensor"),
            P(None, "tensor", "fsdp"),
            P(None, None, "tensor", "fsdp"),
            P(None, "tensor", "fsdp"),
            P(None, None, "fsdp"),
        ),
        out_specs=(
            P("fsdp", None, None),
            P("fsdp", None, None),
            P("fsdp", None, "tensor"),
            P("tensor", "fsdp"),
            P("fsdp", "tensor"),
            P("tensor", "fsdp"),
            P(None, "tensor", "fsdp"),
            P("tensor", "fsdp"),
            P(None, "fsdp"),
            P("fsdp", None, "tensor"),
            P("tensor", "fsdp"),
            P("fsdp", "tensor"),
            P("tensor", "fsdp"),
            P(None, "tensor", "fsdp"),
            P("tensor", "fsdp"),
            P(None, "fsdp"),
            P(None, "fsdp", None, "tensor"),
            P(None, "tensor", "fsdp"),
            P(None, "fsdp", "tensor"),
            P(None, "tensor", "fsdp"),
            P(None, None, "tensor", "fsdp"),
            P(None, "tensor", "fsdp"),
            P(None, None, "fsdp"),
        ),
        check_vma=False,
    )
```
